32 devices in a mesh: dp: 16 (over z, y, x), tensor: 2 (over core).
Axes of the slice: x: 2, y: 2, z: 4, core: 2. Of those that a mesh axis runs over, the one named last changes fastest.
Arguments:
- tokens: bfloat16 [2048, 8192], P('dp', 'tensor'), may hold values from -6 to 6
- gate_left: bfloat16 [8192, 1024], P(None, 'tensor'), may hold values from -0.0625 to 0.0625
- gate_right: bfloat16 [1024, 14336], P(None, 'tensor'), may hold values from -0.1875 to 0.1875
- up_left: bfloat16 [8192, 1024], P(None, 'tensor'), may hold values from -0.0625 to 0.0625
- up_right: bfloat16 [1024, 14336], P(None, 'tensor'), may hold values from -0.1875 to 0.1875
- hidden_grad: bfloat16 [2048, 14336], P('dp', 'tensor'), may hold values from -6 to 6
Outputs:
- input_grad: bfloat16 [2048, 8192], P('dp', 'tensor')
- gate_left_grad: bfloat16 [8192, 1024], P('dp', 'tensor')
- gate_right_grad: bfloat16 [1024, 14336], P('dp', 'tensor')
- up_left_grad: bfloat16 [8192, 1024], P('dp', 'tensor')
- up_right_grad: bfloat16 [1024, 14336], P('dp', 'tensor')
The draws below stay inside these ranges and needn't reach their ends.
All inputs are finite; a program needn't handle non-finite values.
Results may differ from the reference program's by a relative error of at most 0.02.
Values may be sent and summed in bfloat16 or wider, within the bound.
No kernel may reach another device: no remote copies, remote signals or barrier semaphores. Data moves between devices by JAX's collectives and lax.ppermute only.
A program may use at most 256 MiB of HBM per device.

```python
import jax
import jax.numpy as jnp
from jax import lax

D = 8192
FF = 14336
RANK = 1024
TOK_DEV = 128
TOKENS = 2048
N_DP = 16


def raised(values, own_key, source, target, blocks, factor):
    def block_of(dim):
        return (jnp.arange(values.shape[dim]) // (values.shape[dim] // blocks)).reshape((-1,) + (1,) * (values.ndim - 1 - dim))

    first = jax.random.permutation(own_key, blocks)[block_of(target)]
    second = (block_of(target) + blocks // 2) % blocks
    return jnp.where((block_of(source) == first) | (block_of(source) == second), factor * values, values)


def levels(own_key, extent, pieces, least, high):
    factor_of = 1.0
    for dim, blocks in pieces:
        heights = jax.random.uniform(jax.random.fold_in(jax.random.fold_in(own_key, 6), dim), (blocks,), jnp.float32, least / len(pieces), high / len(pieces))
        factor_of = factor_of * jnp.repeat(jnp.exp(heights), extent[dim] // blocks).reshape((-1,) + (1,) * (len(extent) - 1 - dim))
    return factor_of


def gaussian(own_key, dims, spread, reach, shards=(), held_as=jnp.bfloat16):
    loudness = levels(own_key, dims, shards, -0.22, 0.18) if shards else 1.0
    values = jax.random.normal(own_key, dims, jnp.float32) * spread * loudness
    return jnp.minimum(jnp.maximum(values, -reach), reach).astype(held_as)


def bell_draw_with(own_key, extent, width, limit, split, heavy, held_as=jnp.bfloat16):
    values = width * jax.random.normal(own_key, extent, jnp.float32)
    if split:
        values = values * levels(own_key, extent, split, -0.22, 0.18)
    return jnp.clip(raised(values, jax.random.fold_in(own_key, 3), *heavy), -limit, limit).astype(held_as)


def setup_inputs(seed: int = 0) -> dict:
    keys = jax.random.split(jax.random.key(seed), 7)
    return {
        "tokens": bell_draw_with(keys[0], (TOKENS, D), 1.0, 6.0, ((0, 16), (1, 2)), (0, 1, 16, 2.0)),
        "gate_left": gaussian(keys[1], (D, RANK), D ** -0.5, 0.0625, ((1, 2),)),
        "gate_right": gaussian(keys[2], (RANK, FF), RANK ** -0.5, 0.1875, ((1, 2),)),
        "up_left": gaussian(keys[3], (D, RANK), D ** -0.5, 0.0625, ((1, 2),)),
        "up_right": gaussian(keys[4], (RANK, FF), RANK ** -0.5, 0.1875, ((1, 2),)),
        "hidden_grad": gaussian(keys[5], (TOKENS, FF), 1.0, 6.0, ((0, 16), (1, 2))),
    }


def product(left, right, left_dim, right_dim):
    return lax.dot_general(left, right, (((left_dim,), (right_dim,)), ((), ())), preferred_element_type=jnp.float32)


def reference(tokens, gate_left, gate_right, up_left, up_right, hidden_grad):
    loss_scale = float(TOKENS) ** -0.5
    gate_codes = product(tokens, gate_left, 1, 0).astype(jnp.bfloat16)
    up_codes = product(tokens, up_left, 1, 0).astype(jnp.bfloat16)
    gate_pre = product(gate_codes, gate_right, 1, 0)
    up_pre = product(up_codes, up_right, 1, 0)
    sigmoid_gate = jax.nn.sigmoid(gate_pre)
    upstream = hidden_grad.astype(jnp.float32)
    up_delta = (upstream * gate_pre * sigmoid_gate).astype(jnp.bfloat16)
    gate_delta = (upstream * up_pre * sigmoid_gate * (1.0 + gate_pre * (1.0 - sigmoid_gate))).astype(jnp.bfloat16)
    gate_rank = product(gate_delta, gate_right, 1, 1).astype(jnp.bfloat16)
    up_rank = product(up_delta, up_right, 1, 1).astype(jnp.bfloat16)
    input_grad = (product(gate_rank, gate_left, 1, 1) + product(up_rank, up_left, 1, 1)).astype(jnp.bfloat16)
    gate_left_grad = (product(tokens, gate_rank, 0, 0) * loss_scale).astype(jnp.bfloat16)
    up_left_grad = (product(tokens, up_rank, 0, 0) * loss_scale).astype(jnp.bfloat16)

    def accumulate(running, group):
        codes_gate, delta_gate, codes_up, delta_up = group
        term_gate = (product(codes_gate, delta_gate, 0, 0) * loss_scale).astype(jnp.bfloat16)
        term_up = (product(codes_up, delta_up, 0, 0) * loss_scale).astype(jnp.bfloat16)
        term_gate, term_up = lax.optimization_barrier((term_gate, term_up))
        return (running[0] + term_gate.astype(jnp.float32), running[1] + term_up.astype(jnp.float32)), None

    def grouped(array):
        return array.reshape(N_DP, TOK_DEV, array.shape[1])

    empty = jnp.zeros((RANK, FF), jnp.float32)
    sums, unused = lax.scan(accumulate, (empty, empty), (grouped(gate_codes), grouped(gate_delta), grouped(up_codes), grouped(up_delta)))
    return input_grad, gate_left_grad, sums[0].astype(jnp.bfloat16), up_left_grad, sums[1].astype(jnp.bfloat16)
```

```python
import jax
import jax.numpy as jnp
from jax import lax
from jax.sharding import PartitionSpec as P


def product(left, right, left_dim, right_dim):
    return lax.dot_general(
        left, right, (((left_dim,), (right_dim,)), ((), ())), preferred_element_type=jnp.float32
    )


def join(values, axis):
    if lax.axis_size("tensor") != 2:
        return lax.all_gather(values, "tensor", axis=axis, tiled=True)
    other = lax.ppermute(values, "tensor", [(0, 1), (1, 0)])
    first = lax.axis_index("tensor") == 0
    return jnp.where(
        first,
        jnp.concatenate([values, other], axis),
        jnp.concatenate([other, values], axis),
    )


def total(values):
    axis = values.ndim - 1
    if lax.axis_size("tensor") != 2:
        return lax.psum_scatter(values, "tensor", scatter_dimension=axis, tiled=True)
    half = values.shape[-1] // 2
    low, high = values[..., :half], values[..., half:]
    first = lax.axis_index("tensor") == 0
    other = lax.ppermute(jnp.where(first, high, low), "tensor", [(0, 1), (1, 0)])
    kept = jnp.where(first, low, high)
    return (kept.astype(jnp.float32) + other.astype(jnp.float32)).astype(values.dtype)


def exchange(values):
    return lax.all_to_all(values, "dp", split_axis=0, concat_axis=0, tiled=True)


def spread(first, second):
    n = lax.axis_size("dp")
    lines = 4
    plane = n // lines
    both = jnp.stack([first, second])
    groups = [[a * plane + b for a in range(lines)] for b in range(plane)]
    line = lax.all_to_all(
        jnp.broadcast_to(both[None], (lines,) + both.shape),
        "dp",
        split_axis=0,
        concat_axis=0,
        tiled=True,
        axis_index_groups=groups,
    )
    bits = [1 << i for i in range(plane.bit_length() - 1)]
    here = lax.axis_index("dp") % plane
    out = []
    for which, order in ((0, bits), (1, bits[::-1])):
        held = line[:, which][None]
        offsets = [0]
        for bit in order:
            came = lax.ppermute(held, "dp", [(i, i ^ bit) for i in range(n)])
            held = jnp.concatenate([held, came])
            offsets = offsets + [o ^ bit for o in offsets]
        place = jnp.asarray([offsets.index(o) for o in range(plane)])
        blocks = [
            lax.dynamic_index_in_dim(held, place[here ^ b], 0, keepdims=False)
            for b in range(plane)
        ]
        out.append(jnp.stack(blocks, 1).reshape((n,) + first.shape))
    return out


def deltas(gate_pre, up_pre, upstream):
    gate_sig = jax.nn.sigmoid(gate_pre)
    up_delta = (upstream * gate_pre * gate_sig).astype(jnp.bfloat16)
    gate_delta = (
        upstream * up_pre * gate_sig * (1.0 + gate_pre * (1.0 - gate_sig))
    ).astype(jnp.bfloat16)
    return gate_delta, up_delta


def body(tokens, gate_left, gate_right, up_left, up_right, hidden_grad):
    n, cores = lax.axis_size("dp"), lax.axis_size("tensor")
    here, core = lax.axis_index("dp"), lax.axis_index("tensor")
    rows, units = hidden_grad.shape
    rank = gate_right.shape[0]
    loss_scale = float(rows * n) ** (-0.5)

    share = units // n
    hidden_all = exchange(hidden_grad.reshape(rows, n, share).transpose(1, 0, 2))
    hidden_all = hidden_all.reshape(rows * n, share)

    gathered = join(tokens, 1)
    features = gathered.shape[1]
    mine = gathered.reshape(rows, n, cores, features // n // cores)
    mine = lax.dynamic_index_in_dim(mine, core, 2, keepdims=False).transpose(1, 0, 2)

    gate_part = product(gathered, gate_left, 1, 0).astype(jnp.bfloat16)
    up_part = product(gathered, up_left, 1, 0).astype(jnp.bfloat16)
    gate_codes, up_codes = join(gate_part, 1), join(up_part, 1)
    gate_every, up_every = spread(gate_part, up_part)

    gate_delta, up_delta = deltas(
        product(gate_codes, gate_right, 1, 0),
        product(up_codes, up_right, 1, 0),
        hidden_grad.astype(jnp.float32),
    )
    gate_rank = total(product(gate_delta, gate_right, 1, 1).astype(jnp.bfloat16))
    up_rank = total(product(up_delta, up_right, 1, 1).astype(jnp.bfloat16))
    input_terms = product(gate_rank, gate_left, 1, 1) + product(up_rank, up_left, 1, 1)
    input_grad = total(input_terms.astype(jnp.bfloat16))

    tokens_all = join(exchange(mine), 2).reshape(rows * n, features // n)
    gate_rank_all, up_rank_all = spread(gate_rank, up_rank)
    gate_left_grad = product(tokens_all, gate_rank_all.reshape(rows * n, -1), 0, 0) * loss_scale
    up_left_grad = product(tokens_all, up_rank_all.reshape(rows * n, -1), 0, 0) * loss_scale

    gate_every = join(gate_every, 2).reshape(rows * n, rank)
    up_every = join(up_every, 2).reshape(rows * n, rank)
    gate_slice = lax.dynamic_slice_in_dim(gate_right, here * share, share, 1)
    up_slice = lax.dynamic_slice_in_dim(up_right, here * share, share, 1)
    gate_delta, up_delta = deltas(
        product(gate_every, gate_slice, 1, 0),
        product(up_every, up_slice, 1, 0),
        hidden_all.astype(jnp.float32),
    )
    gate_grad = (product(gate_every, gate_delta, 0, 0) * loss_scale).astype(jnp.bfloat16)
    up_grad = (product(up_every, up_delta, 0, 0) * loss_scale).astype(jnp.bfloat16)
    gate_grad = exchange(gate_grad.reshape(n, rank // n, share))
    up_grad = exchange(up_grad.reshape(n, rank // n, share))

    return (
        input_grad,
        gate_left_grad.astype(jnp.bfloat16),
        gate_grad.transpose(1, 0, 2).reshape(rank // n, units),
        up_left_grad.astype(jnp.bfloat16),
        up_grad.transpose(1, 0, 2).reshape(rank // n, units),
    )


def solution(mesh):
    placed = (
        P("dp", "tensor"),
        P(None, "tensor"),
        P(None, "tensor"),
        P(None, "tensor"),
        P(None, "tensor"),
        P("dp", "tensor"),
    )
    return jax.shard_map(
        body,
        mesh=mesh,
        in_specs=placed,
        out_specs=(P("dp", "tensor"),) * 5,
        check_vma=False,
    )
```

```python
import functools

import jax
import jax.numpy as jnp
from jax import lax
from jax.experimental import pallas as pl
from jax.experimental.pallas import tpu as pltpu
from jax.sharding import PartitionSpec as P

LINES = 4


def product(left, right, left_dim, right_dim):
    return lax.dot_general(
        left, right, (((left_dim,), (right_dim,)), ((), ())), preferred_element_type=jnp.float32
    )


def join(values, axis):
    if lax.axis_size("tensor") != 2:
        return lax.all_gather(values, "tensor", axis=axis, tiled=True)
    other = lax.ppermute(values, "tensor", [(0, 1), (1, 0)])
    first = lax.axis_index("tensor") == 0
    return jnp.where(
        first,
        jnp.concatenate([values, other], axis),
        jnp.concatenate([other, values], axis),
    )


def total(values):
    axis = values.ndim - 1
    if lax.axis_size("tensor") != 2:
        return lax.psum_scatter(values, "tensor", scatter_dimension=axis, tiled=True)
    half = values.shape[-1] // 2
    low, high = values[..., :half], values[..., half:]
    first = lax.axis_index("tensor") == 0
    other = lax.ppermute(jnp.where(first, high, low), "tensor", [(0, 1), (1, 0)])
    kept = jnp.where(first, low, high)
    return (kept.astype(jnp.float32) + other.astype(jnp.float32)).astype(values.dtype)


def exchange(values):
    return lax.all_to_all(values, "dp", split_axis=0, concat_axis=0, tiled=True)


def spread(first, second):
    n = lax.axis_size("dp")
    lines = LINES
    plane = n // lines
    both = jnp.stack([first, second])
    groups = [[a * plane + b for a in range(lines)] for b in range(plane)]
    line = lax.all_to_all(
        jnp.broadcast_to(both[None], (lines,) + both.shape),
        "dp",
        split_axis=0,
        concat_axis=0,
        tiled=True,
        axis_index_groups=groups,
    )
    bits = [1 << i for i in range(plane.bit_length() - 1)]
    here = lax.axis_index("dp") % plane
    out = []
    for which, order in ((0, bits), (1, bits[::-1])):
        held = line[:, which][None]
        offsets = [0]
        for bit in order:
            came = lax.ppermute(held, "dp", [(i, i ^ bit) for i in range(n)])
            held = jnp.concatenate([held, came])
            offsets = offsets + [o ^ bit for o in offsets]
        place = jnp.asarray([offsets.index(o) for o in range(plane)])
        blocks = [
            lax.dynamic_index_in_dim(held, place[here ^ b], 0, keepdims=False)
            for b in range(plane)
        ]
        out.append(jnp.stack(blocks, 1).reshape((n,) + first.shape))
    return out


def deltas(gate_pre, up_pre, upstream):
    gate_sig = jax.nn.sigmoid(gate_pre)
    up_delta = (upstream * gate_pre * gate_sig).astype(jnp.bfloat16)
    gate_delta = (
        upstream * up_pre * gate_sig * (1.0 + gate_pre * (1.0 - gate_sig))
    ).astype(jnp.bfloat16)
    return gate_delta, up_delta


def general(tokens, gate_left, gate_right, up_left, up_right, hidden_grad):
    n, cores = lax.axis_size("dp"), lax.axis_size("tensor")
    here, core = lax.axis_index("dp"), lax.axis_index("tensor")
    rows, units = hidden_grad.shape
    rank = gate_right.shape[0]
    loss_scale = float(rows * n) ** (-0.5)

    share = units // n
    hidden_all = exchange(hidden_grad.reshape(rows, n, share).transpose(1, 0, 2))
    hidden_all = hidden_all.reshape(rows * n, share)

    gathered = join(tokens, 1)
    features = gathered.shape[1]
    mine = gathered.reshape(rows, n, cores, features // n // cores)
    mine = lax.dynamic_index_in_dim(mine, core, 2, keepdims=False).transpose(1, 0, 2)

    gate_part = product(gathered, gate_left, 1, 0).astype(jnp.bfloat16)
    up_part = product(gathered, up_left, 1, 0).astype(jnp.bfloat16)
    gate_codes, up_codes = join(gate_part, 1), join(up_part, 1)
    gate_every, up_every = spread(gate_part, up_part)

    gate_delta, up_delta = deltas(
        product(gate_codes, gate_right, 1, 0),
        product(up_codes, up_right, 1, 0),
        hidden_grad.astype(jnp.float32),
    )
    gate_rank = total(product(gate_delta, gate_right, 1, 1).astype(jnp.bfloat16))
    up_rank = total(product(up_delta, up_right, 1, 1).astype(jnp.bfloat16))
    input_terms = product(gate_rank, gate_left, 1, 1) + product(up_rank, up_left, 1, 1)
    input_grad = total(input_terms.astype(jnp.bfloat16))

    tokens_all = join(exchange(mine), 2).reshape(rows * n, features // n)
    gate_rank_all, up_rank_all = spread(gate_rank, up_rank)
    gate_left_grad = product(tokens_all, gate_rank_all.reshape(rows * n, -1), 0, 0) * loss_scale
    up_left_grad = product(tokens_all, up_rank_all.reshape(rows * n, -1), 0, 0) * loss_scale

    gate_every = join(gate_every, 2).reshape(rows * n, rank)
    up_every = join(up_every, 2).reshape(rows * n, rank)
    gate_slice = lax.dynamic_slice_in_dim(gate_right, here * share, share, 1)
    up_slice = lax.dynamic_slice_in_dim(up_right, here * share, share, 1)
    gate_delta, up_delta = deltas(
        product(gate_every, gate_slice, 1, 0),
        product(up_every, up_slice, 1, 0),
        hidden_all.astype(jnp.float32),
    )
    gate_grad = (product(gate_every, gate_delta, 0, 0) * loss_scale).astype(jnp.bfloat16)
    up_grad = (product(up_every, up_delta, 0, 0) * loss_scale).astype(jnp.bfloat16)
    gate_grad = exchange(gate_grad.reshape(n, rank // n, share))
    up_grad = exchange(up_grad.reshape(n, rank // n, share))

    return (
        input_grad,
        gate_left_grad.astype(jnp.bfloat16),
        gate_grad.transpose(1, 0, 2).reshape(rank // n, units),
        up_left_grad.astype(jnp.bfloat16),
        up_grad.transpose(1, 0, 2).reshape(rank // n, units),
    )


def pair(values):
    return lax.ppermute(values, "tensor", [(0, 1), (1, 0)])


def local_kernel(core_ref, own_ref, other_ref, gate_w_ref, up_w_ref, hidden_ref, keep_ref, send_ref, codes, sums):
    step = pl.program_id(0)
    core = core_ref[0]
    half = own_ref.shape[2]

    @pl.when(step == 0)
    def _():
        sums[...] = jnp.zeros_like(sums)
        codes[core] = own_ref[...]
        codes[1 - core] = other_ref[...]

    gate_w, up_w = gate_w_ref[...], up_w_ref[...]
    gate_pre = jnp.dot(codes[0, 0], gate_w[:half], preferred_element_type=jnp.float32)
    gate_pre += jnp.dot(codes[1, 0], gate_w[half:], preferred_element_type=jnp.float32)
    up_pre = jnp.dot(codes[0, 1], up_w[:half], preferred_element_type=jnp.float32)
    up_pre += jnp.dot(codes[1, 1], up_w[half:], preferred_element_type=jnp.float32)
    gate_delta, up_delta = deltas(gate_pre, up_pre, hidden_ref[...].astype(jnp.float32))
    for which, delta, weight in ((0, gate_delta, gate_w), (1, up_delta, up_w)):
        for side in range(2):
            sums[side, which] += product(delta, weight[side * half : (side + 1) * half], 1, 1)

    @pl.when(step == pl.num_programs(0) - 1)
    def _():
        keep_ref[...] = sums[core]
        send_ref[...] = sums[1 - core].astype(send_ref.dtype)


def local_ranks(core, own, other, gate_right, up_right, hidden_grad, block):
    rank, units = gate_right.shape
    rows = hidden_grad.shape[0]
    whole = pl.BlockSpec(own.shape, lambda i, c: (0, 0, 0))
    weight = pl.BlockSpec((rank, block), lambda i, c: (0, i))
    return pl.pallas_call(
        local_kernel,
        name="local_ranks",
        out_shape=(
            jax.ShapeDtypeStruct(own.shape, jnp.float32),
            jax.ShapeDtypeStruct(own.shape, jnp.bfloat16),
        ),
        grid_spec=pltpu.PrefetchScalarGridSpec(
            num_scalar_prefetch=1,
            grid=(units // block,),
            in_specs=[whole, whole, weight, weight, pl.BlockSpec((rows, block), lambda i, c: (0, i))],
            out_specs=[whole, whole],
            scratch_shapes=[
                pltpu.VMEM((2,) + own.shape, jnp.bfloat16),
                pltpu.VMEM((2,) + own.shape, jnp.float32),
            ],
        ),
        compiler_params=pltpu.CompilerParams(dimension_semantics=("arbitrary",)),
        cost_estimate=pl.CostEstimate(
            flops=8 * rows * rank * units,
            transcendentals=2 * rows * units,
            bytes_accessed=4 * rank * units + 2 * rows * units,
        ),
    )(core[None], own, other, gate_right, up_right, hidden_grad)


def weights_kernel(where_ref, gate_ref, up_ref, out_ref, window, sems):
    core, shift = where_ref[0], where_ref[2]
    width = window.shape[2]
    half, share = out_ref.shape[2] // 2, out_ref.shape[1]
    start = pl.multiple_of(where_ref[1], 128)
    copies = [
        pltpu.make_async_copy(ref.at[:, pl.ds(start, width)], window.at[i], sems.at[i])
        for i, ref in enumerate((gate_ref, up_ref))
    ]
    for copy in copies:
        copy.start()
    for i, copy in enumerate(copies):
        copy.wait()
        for side in range(2):
            first = pl.multiple_of((core if side == 0 else 1 - core) * half, half)
            turned = window[i, pl.ds(first, half), :].T
            low, high = turned[:share], turned[width - share :]
            out_ref[i, :, side * half : (side + 1) * half] = jnp.where(shift == 0, low, high)


def weight_slices(core, here, gate_right, up_right, share):
    rank = gate_right.shape[0]
    width = -(-share // 128) * 128
    start = here * share
    where = jnp.stack([core, start // 128 * 128, start % 128]).astype(jnp.int32)
    return pl.pallas_call(
        weights_kernel,
        name="weight_slices",
        out_shape=jax.ShapeDtypeStruct((2, share, rank), jnp.bfloat16),
        in_specs=[
            pl.BlockSpec(memory_space=pltpu.SMEM),
            pl.BlockSpec(memory_space=pl.ANY),
            pl.BlockSpec(memory_space=pl.ANY),
        ],
        out_specs=pl.BlockSpec(memory_space=pltpu.VMEM),
        scratch_shapes=[
            pltpu.VMEM((2, rank, width), jnp.bfloat16),
            pltpu.SemaphoreType.DMA((2,)),
        ],
        cost_estimate=pl.CostEstimate(
            flops=0, transcendentals=0, bytes_accessed=8 * rank * share
        ),
    )(where, gate_right, up_right)


def pack_kernel(core_ref, own_ref, other_ref, out_ref):
    core = core_ref[0]
    blocks, width = out_ref.shape[:2]
    from_own = (pl.program_id(0) >= pl.num_programs(0) // 2) == (core == 1)

    def move(source):
        for i in range(blocks):
            first = pl.multiple_of((2 * i + core) * width, width)
            out_ref[i] = source[:, pl.ds(first, width)].T

    pl.when(from_own)(lambda: move(own_ref))
    pl.when(jnp.logical_not(from_own))(lambda: move(other_ref))


def pack_tokens(core, own, other, n):
    rows, local = own.shape
    width = local // n
    steps = 4
    block = pl.BlockSpec((rows, 2 * local // steps), lambda i, c: (0, i % (steps // 2)))
    return pl.pallas_call(
        pack_kernel,
        name="pack_tokens",
        out_shape=jax.ShapeDtypeStruct((n, width, rows), own.dtype),
        grid_spec=pltpu.PrefetchScalarGridSpec(
            num_scalar_prefetch=1,
            grid=(steps,),
            in_specs=[block, block],
            out_specs=pl.BlockSpec((n // steps, width, rows), lambda i, c: (i, 0, 0)),
        ),
        cost_estimate=pl.CostEstimate(
            flops=0, transcendentals=0, bytes_accessed=6 * rows * local
        ),
    )(core[None], own, other)


def right_kernel(scale, first, last, where_ref, *refs):
    if last:
        sides = ((refs[0], refs[2]), (refs[1], refs[3]))
        read = lambda ref, i: ref[...]
        rest = refs[4:]
    else:
        sides = (refs[:2], refs[:2])
        read = lambda ref, i: ref[i]
        rest = refs[2:]
    hidden, weights = rest[:2]
    held = None if first else rest[2]
    out = refs[-1]
    share, half = weights.shape[1], weights.shape[2] // 2
    lines = hidden.shape[0]
    codes = [
        jnp.concatenate([read(ref, i).reshape(-1, half) for ref in sides[i]], 1) for i in range(2)
    ]
    gate_pre, up_pre = [product(weights[i], codes[i], 1, 1) for i in range(2)]
    block = where_ref[1]
    upstream = jnp.concatenate(
        [hidden[(where_ref[2] + lines - i) % lines, block] for i in range(lines)], 1
    ).astype(jnp.float32)
    both = deltas(gate_pre, up_pre, upstream)
    for side in range(2):
        parts = []
        for i in range(2):
            term = product(both[i], codes[i][:, side * half : (side + 1) * half], 1, 0)
            if not first:
                term += held[side, i * share : (i + 1) * share]
            if last:
                parts.append(term * scale)
            else:
                out[side, i * share : (i + 1) * share] = term
        if last:
            done = jnp.concatenate(parts, 0).T.astype(out.dtype)
            place = where_ref[0] if side == 0 else 1 - where_ref[0]
            blocks = out.shape[0] // 2
            out[pl.ds(place * blocks, blocks)] = done.reshape((blocks,) + out.shape[1:])


def right_part(where, pieces, sums, last, hidden, weights, scale, n):
    share, half = weights.shape[1], weights.shape[2] // 2
    lines, rows = hidden.shape[0], hidden.shape[3]
    vmem = pl.BlockSpec(memory_space=pltpu.VMEM)
    operands = list(pieces) + [hidden, weights] + ([] if sums is None else [sums])
    if last:
        out_shape = jax.ShapeDtypeStruct((n, 2 * half // n, 2 * share), jnp.bfloat16)
    else:
        out_shape = jax.ShapeDtypeStruct((2, 2 * share, half), jnp.float32)
    return pl.pallas_call(
        functools.partial(right_kernel, scale, sums is None, last),
        name="right_last" if last else "right_part",
        out_shape=out_shape,
        in_specs=[pl.BlockSpec(memory_space=pltpu.SMEM)] + [vmem] * len(operands),
        out_specs=vmem,
        input_output_aliases={} if sums is None or last else {5: 0},
        cost_estimate=pl.CostEstimate(
            flops=16 * lines * rows * half * share,
            transcendentals=2 * lines * rows * share,
            bytes_accessed=8 * lines * rows * half + 8 * share * half,
        ),
    )(where, *operands)


def settle_kernel(in_ref, gate_ref, up_ref):
    width = in_ref.shape[2]
    first = lax.broadcasted_iota(jnp.int32, in_ref.shape[1:], 1) < width // 2
    for i in range(in_ref.shape[0] // 2):
        even, odd = in_ref[2 * i].astype(jnp.float32), in_ref[2 * i + 1].astype(jnp.float32)
        columns = slice(i * width, (i + 1) * width)
        gate = jnp.where(first, even, pltpu.roll(odd, width // 2, 1))
        up = jnp.where(first, pltpu.roll(even, width // 2, 1), odd)
        gate_ref[:, columns] = gate.astype(gate_ref.dtype)
        up_ref[:, columns] = up.astype(up_ref.dtype)


def settle(blocks):
    n, rows, width = blocks.shape
    vmem = pl.BlockSpec(memory_space=pltpu.VMEM)
    shape = jax.ShapeDtypeStruct((rows, n * width // 2), blocks.dtype)
    return pl.pallas_call(
        settle_kernel,
        name="settle",
        out_shape=(shape, shape),
        in_specs=[vmem],
        out_specs=(vmem, vmem),
        cost_estimate=pl.CostEstimate(
            flops=0, transcendentals=0, bytes_accessed=4 * n * rows * width
        ),
    )(blocks)


def input_kernel(core_ref, ranks_ref, gate_ref, up_ref, send_ref, keep_ref):
    step = pl.program_id(0)
    half = pl.num_programs(0) // 2
    terms = product(ranks_ref[0], gate_ref[...], 1, 1) + product(ranks_ref[1], up_ref[...], 1, 1)

    @pl.when(step < half)
    def _():
        send_ref[...] = terms.astype(send_ref.dtype)

    @pl.when(step >= half)
    def _():
        keep_ref[...] = terms


def input_terms(core, ranks, gate_left, up_left):
    features, half = gate_left.shape
    rows = ranks.shape[1]
    steps = 8
    block = features // steps
    weight = pl.BlockSpec((block, half), lambda i, c: ((i + (1 - c[0]) * (steps // 2)) % steps, 0))
    return pl.pallas_call(
        input_kernel,
        name="input_terms",
        out_shape=(
            jax.ShapeDtypeStruct((rows, features // 2), jnp.bfloat16),
            jax.ShapeDtypeStruct((rows, features // 2), jnp.float32),
        ),
        grid_spec=pltpu.PrefetchScalarGridSpec(
            num_scalar_prefetch=1,
            grid=(steps,),
            in_specs=[pl.BlockSpec(ranks.shape, lambda i, c: (0, 0, 0)), weight, weight],
            out_specs=[
                pl.BlockSpec((rows, block), lambda i, c: (0, jnp.minimum(i, steps // 2 - 1))),
                pl.BlockSpec((rows, block), lambda i, c: (0, jnp.maximum(i - steps // 2, 0))),
            ],
        ),
        compiler_params=pltpu.CompilerParams(dimension_semantics=("arbitrary",)),
        cost_estimate=pl.CostEstimate(
            flops=4 * rows * half * features,
            transcendentals=0,
            bytes_accessed=4 * half * features + 6 * rows * features // 2,
        ),
    )(core[None], ranks, gate_left, up_left)


def left_kernel(scale, where_ref, own, other, *refs):
    pieces, (gate_out, up_out) = refs[:-2], refs[-2:]
    core = where_ref[0]
    lines, half = pieces[0].shape[1], pieces[0].shape[3]
    width = own.shape[2]
    ranks = [[piece[i] for piece in pieces[:3]] + [pieces[3 + i][...]] for i in range(2)]
    for side, source in ((0, own), (1, other)):
        sums = [0.0, 0.0]
        for offset in range(4):
            block = where_ref[1] ^ offset
            values = jnp.concatenate(
                [source[(where_ref[2] + lines - i) % lines, block] for i in range(lines)], 1
            )
            for i in range(2):
                sums[i] += product(values, ranks[i][offset].reshape(-1, half), 1, 0)
        start = pl.multiple_of((core if side == 0 else 1 - core) * width, width)
        for out, result in ((gate_out, sums[0]), (up_out, sums[1])):
            out[pl.ds(start, width), :] = (result * scale).astype(out.dtype)


def left_grads(where, own, other, pieces, scale):
    width, half = own.shape[2], pieces[0].shape[3]
    vmem = pl.BlockSpec(memory_space=pltpu.VMEM)
    shape = jax.ShapeDtypeStruct((2 * width, half), jnp.bfloat16)
    tokens = own.shape[0] * own.shape[1] * own.shape[3]
    return pl.pallas_call(
        functools.partial(left_kernel, scale),
        name="left_grads",
        out_shape=(shape, shape),
        in_specs=[pl.BlockSpec(memory_space=pltpu.SMEM)] + [vmem] * (2 + len(pieces)),
        out_specs=(vmem, vmem),
        cost_estimate=pl.CostEstimate(
            flops=8 * width * half * tokens,
            transcendentals=0,
            bytes_accessed=4 * width * tokens + 4 * half * tokens,
        ),
    )(where, own, other, *pieces)


def line_gather(values):
    n = lax.axis_size("dp")
    plane = n // LINES
    return [values] + [
        lax.ppermute(values, "dp", [(i, (i + shift * plane) % n) for i in range(n)])
        for shift in range(1, LINES)
    ]


def stacked(line):
    return jnp.stack([jnp.stack([values[i] for values in line]) for i in range(2)])


def hop(values, bit):
    return lax.ppermute(values, "dp", [(i, i ^ bit) for i in range(lax.axis_size("dp"))])


def after(value, *others):
    return lax.optimization_barrier((value, *others))[0]


def fast(tokens, gate_left, gate_right, up_left, up_right, hidden_grad):
    n = lax.axis_size("dp")
    here, core = lax.axis_index("dp"), lax.axis_index("tensor")
    rows, units = hidden_grad.shape
    share, plane = units // n, n // LINES
    scale = float(rows * n) ** (-0.5)
    where = [
        jnp.stack([core, (here % plane) ^ offset, here // plane]).astype(jnp.int32)
        for offset in range(plane)
    ]

    hidden_all = exchange(hidden_grad.T.reshape(n, share, rows)).reshape(LINES, plane, share, rows)

    other = pair(tokens)
    gathered = jnp.where(
        core == 0,
        jnp.concatenate([tokens, other], 1),
        jnp.concatenate([other, tokens], 1),
    )
    parts = jnp.stack(
        [
            product(gathered, gate_left, 1, 0).astype(jnp.bfloat16),
            product(gathered, up_left, 1, 0).astype(jnp.bfloat16),
        ]
    )
    line = line_gather(parts)
    packed = pack_tokens(core, tokens, other, n)
    weights = weight_slices(core, here, gate_right, up_right, share)

    parts_other = pair(parts)
    keep, send = local_ranks(
        core, after(parts, packed, weights), parts_other, gate_right, up_right, hidden_grad, 512
    )
    own = stacked(after(line, keep))
    ranks = (keep + pair(send).astype(jnp.float32)).astype(jnp.bfloat16)

    codes_x, codes_y, own_pair = hop(own, 1), hop(own, 2), pair(own)
    rank_line = line_gather(after(ranks, own_pair))
    send, keep = input_terms(core, after(ranks, own_pair), gate_left, up_left)
    input_pair = pair(send)
    mine = exchange(after(packed, keep))

    part = functools.partial(right_part, hidden=hidden_all, weights=weights, scale=scale, n=n)
    sums = part(where[0], (after(own, keep), own_pair), sums=None, last=False)
    codes_x, codes_y, rank_line, sums = lax.optimization_barrier(
        (codes_x, codes_y, rank_line, sums)
    )
    gate_xy, up_xy = hop(codes_x[0], 2), hop(codes_y[1], 1)
    x_pair, y_pair = pair(codes_x), pair(codes_y)
    rank_own = stacked(rank_line)
    rank_x, rank_y = hop(rank_own, 1), hop(rank_own, 2)
    sums = part(where[1], (codes_x, x_pair), sums=sums, last=False)
    sums = part(where[2], (codes_y, y_pair), sums=sums, last=False)
    gate_xy, up_xy, sums = lax.optimization_barrier((gate_xy, up_xy, sums))
    pieces = (gate_xy, up_xy, pair(gate_xy), pair(up_xy))
    sums = part(where[3], pieces, sums=sums, last=True)
    rank_x, rank_y, sums = lax.optimization_barrier((rank_x, rank_y, sums))
    gate_xy, up_xy = hop(rank_x[0], 2), hop(rank_y[1], 1)
    finished = exchange(sums)

    input_grad = (keep + input_pair.astype(jnp.float32)).astype(jnp.bfloat16)
    mine = mine.reshape((LINES, plane) + packed.shape[1:])
    gate_left_grad, up_left_grad = left_grads(
        where[0], mine, pair(mine), (rank_own, rank_x, rank_y, gate_xy, up_xy), scale
    )
    gate_grad, up_grad = settle(finished)
    return input_grad, gate_left_grad, gate_grad, up_left_grad, up_grad


def body(tokens, gate_left, gate_right, up_left, up_right, hidden_grad):
    n, cores = lax.axis_size("dp"), lax.axis_size("tensor")
    fits = n == 4 * LINES and cores == 2 and tokens.shape[0] % 128 == 0
    fits = fits and hidden_grad.shape[1] % (n * 16) == 0 and hidden_grad.shape[1] % 512 == 0
    fits = fits and gate_left.shape[1] % 128 == 0 and gate_left.shape[0] % (n * 256) == 0
    fits = fits and hidden_grad.shape[1] // n % 128 in (0, 64)
    chosen = fast if fits else general
    return chosen(tokens, gate_left, gate_right, up_left, up_right, hidden_grad)


def solution(mesh):
    placed = (
        P("dp", "tensor"),
        P(None, "tensor"),
        P(None, "tensor"),
        P(None, "tensor"),
        P(None, "tensor"),
        P("dp", "tensor"),
    )
    return jax.shard_map(
        body,
        mesh=mesh,
        in_specs=placed,
        out_specs=(P("dp", "tensor"),) * 5,
        check_vma=False,
    )
```
